32 devices in a mesh: pair: 8 (over z, x), col: 4 (over y, core).
Axes of the slice: x: 2, y: 2, z: 4, core: 2. Of those that a mesh axis runs over, the one named last changes fastest.
Arguments:
- left_tiles: bfloat16 [96, 64, 4096], P('pair'), may hold values from -0.21875 to 0.21875
- left_row: int32 [96], P('pair'), may hold values from 0 to 71
- left_lam: int32 [96], P('pair'), may hold values from 0 to 7
- left_count: int32 [8], P('pair'), may hold values from 1 to 12, as said below
- density: bfloat16 [36864, 256], P('pair', 'col'), may hold values from -6 to 6
- metric: float32 [64, 64], replicated, as said below
- back_tiles: bfloat16 [36864, 16384], P('pair', 'col'), may hold values from -0.046875 to 0.046875
- back_pattern: int32 [576, 4], P('pair', 'col'), may hold values 0 or 1
Outputs:
- exchange_block: float32 [512, 36864], P('col', 'pair')
The draws below stay inside these ranges and needn't reach their ends.
Inputs may be any that keep to these rules, and one draw needn't show every extreme that they name: `left_count`: slots at or past a device's count are unused; some index of pair has all 12 slots live. `metric`: symmetric.
All inputs are finite; a program needn't handle non-finite values. No bound on the sum of `back_pattern` on one device may be relied on, other than what follows from the above.
Results may differ from the reference program's by a relative error of at most 0.0029.
Values may be sent and summed in bfloat16 or wider, within the bound.
No kernel may reach another device: no remote copies, remote signals or barrier semaphores. Data moves between devices by JAX's collectives and lax.ppermute only.
A program may use at most 128 MiB of HBM per device.

```python
import math
import jax
import jax.numpy as jnp
from jax import lax

BLK = 64
AUX = 64
NBLK = 576
LW = 8
TL_CAP = 12
BASIS = 36864
MB_DEV = 72
TILES = 96
SIGMA = 256
N_PAIR = 8
N_COL = 4


def draw_left_count(key, part):
    first_key, second_key = jax.random.split(jax.random.fold_in(key, 7))
    lowest = max(1, TL_CAP // 4)
    counts = jax.random.randint(first_key, (N_PAIR,), lowest, TL_CAP + 1)
    filled = jax.random.randint(second_key, (), 0, N_PAIR)
    return jnp.where(jnp.arange(N_PAIR) == filled, TL_CAP, counts).astype(jnp.int32)


def draw_metric(key, part):
    first_key, second_key = jax.random.split(jax.random.fold_in(key, 11), 2)
    diagonal = jnp.exp(jax.random.uniform(first_key, (AUX,), jnp.float32, math.log(0.5), math.log(2.0)))
    random_part = jax.random.normal(second_key, (AUX, AUX), jnp.float32)
    symmetric = (random_part + random_part.T) * (0.5 / math.sqrt(AUX))
    return (jnp.diag(diagonal) + symmetric).astype(jnp.float32)


def with_ends(values, rng, smallest, top_value):
    longest = values.shape.index(max(values.shape))
    spots = []
    for shift in (0, 1):
        where = [jax.random.randint(jax.random.fold_in(rng, axis), (), 0, length) for axis, length in enumerate(values.shape)]
        where[longest] = (where[longest] + shift) % values.shape[longest]
        spots.append(tuple(where))
    return values.at[spots[0]].set(smallest).at[spots[1]].set(top_value)


def shard_levels(key, extent, shards, least, high):
    def one(dim, shards_of):
        draws = jax.random.uniform(jax.random.fold_in(jax.random.fold_in(key, 6), dim), (shards_of,), jnp.float32, least / len(shards), high / len(shards))
        return jnp.repeat(jnp.exp(draws), extent[dim] // shards_of).reshape((-1,) + (1,) * (len(extent) - dim - 1))

    level = one(*shards[0])
    for cut in shards[1:]:
        level = level * one(*cut)
    return level


def gaussian(key, extent, deviation, bound, pieces=(), held_as=jnp.bfloat16):
    drawn = deviation * jax.random.normal(key, extent, jnp.float32)
    if pieces:
        drawn = drawn * shard_levels(key, extent, pieces, -0.22, 0.18)
    return jnp.clip(drawn, -bound, bound).astype(held_as)


def setup_inputs(seed: int = 0) -> dict:
    splits = jax.random.split(jax.random.key(seed), 9)
    left_tiles = gaussian(splits[0], (TILES, BLK, BLK * AUX), (BLK * N_PAIR * TL_CAP // LW) ** -0.5, 0.21875, ((0, 8),))
    left_row = with_ends(jax.random.randint(splits[1], (TILES,), 0, MB_DEV), jax.random.fold_in(splits[1], 1), 0, MB_DEV - 1).astype(jnp.int32)
    left_lam = with_ends(jax.random.randint(splits[2], (TILES,), 0, LW), jax.random.fold_in(splits[2], 1), 0, LW - 1).astype(jnp.int32)
    left_count = draw_left_count(jax.random.fold_in(splits[8], 71), 0)
    density = gaussian(splits[4], (BASIS, SIGMA), 1.0, 6.0, ((0, 8), (1, 4)))
    metric = draw_metric(jax.random.fold_in(splits[8], 71), 0)
    back_tiles = gaussian(splits[6], (BASIS, SIGMA * AUX), (BLK * AUX * N_COL) ** -0.5, 0.046875, ((0, 8), (1, 4)))
    back_pattern = with_ends((jax.random.randint(splits[7], (NBLK, N_COL), 0, 4) < 3).astype(jnp.int32), jax.random.fold_in(splits[7], 1), 0, 1)
    return {"left_tiles": left_tiles, "left_row": left_row, "left_lam": left_lam, "left_count": left_count, "density": density, "metric": metric, "back_tiles": back_tiles, "back_pattern": back_pattern}


def reference(left_tiles, left_row, left_lam, left_count, density, metric, back_tiles, back_pattern):
    slot_ids = jnp.arange(TILES, dtype=jnp.int32)
    owners = (slot_ids // TL_CAP).astype(jnp.int32)
    alive_slots = ((slot_ids % TL_CAP) < left_count[owners]).astype(jnp.float32)
    mu_blocks = (owners * MB_DEV + left_row).astype(jnp.int32)
    initial = jnp.zeros((LW * BLK, SIGMA * AUX), jnp.float32)

    def add_tile(running, inputs):
        tile_block, mu_block, lam_block, weight = inputs
        dens_rows = lax.dynamic_slice_in_dim(density, (mu_block * BLK).astype(jnp.int32), BLK, 0)
        contrib = jnp.einsum("mlp,ms->lsp", tile_block.reshape(BLK, BLK, AUX).astype(jnp.float32), dens_rows.astype(jnp.float32))
        contrib = contrib.reshape(BLK, SIGMA * AUX) * weight
        target = (lam_block * BLK).astype(jnp.int32)
        current = lax.dynamic_slice_in_dim(running, target, BLK, 0)
        return lax.dynamic_update_slice_in_dim(running, current + contrib, target, 0), weight

    summed, unused = lax.scan(add_tile, initial, (left_tiles, mu_blocks, left_lam, alive_slots))
    applied = jnp.dot(summed.reshape(-1, AUX), metric, precision=lax.Precision.HIGHEST, preferred_element_type=jnp.float32)
    applied = applied.reshape(LW * BLK, SIGMA * AUX).astype(jnp.bfloat16)
    exchange = jnp.zeros((LW * BLK, BASIS), jnp.float32)
    for column in range(N_COL):
        first_col = column * BLK * AUX
        mixed_block = applied[:, first_col:first_col + BLK * AUX]
        back_block = back_tiles[:, first_col:first_col + BLK * AUX]
        pattern_cols = jnp.repeat(back_pattern[:, column], BLK).astype(jnp.float32)
        exchange = exchange + jnp.dot(mixed_block, back_block.T, preferred_element_type=jnp.float32) * pattern_cols[None, :]
    return exchange
```

```python
import functools

import jax
import jax.numpy as jnp
from jax import lax
from jax.experimental import pallas as pl
from jax.experimental.pallas import tpu as pltpu
from jax.sharding import PartitionSpec as P

LW = 8
INNER = 2
CHUNKS = 2
LANES = 128
F32 = jnp.float32
BF16 = jnp.bfloat16
I16 = jnp.int16


def apply_metric(summed, metric, aux_size):
    flattened = summed.reshape(-1, aux_size)
    product = jnp.dot(
        flattened, metric, precision=lax.Precision.HIGHEST, preferred_element_type=F32
    )
    return product.reshape(summed.shape).astype(BF16)


def general(
    left_tiles, left_row, left_lam, left_count, density, metric, back_tiles, back_pattern
):
    block_size = left_tiles.shape[1]
    aux_size = left_tiles.shape[2] // block_size
    window_rows = LW * block_size
    live_count = left_count[0]

    def add_tile(slot_index, running):
        tile_block = lax.dynamic_index_in_dim(left_tiles, slot_index, 0, keepdims=False)
        row_first = left_row[slot_index] * block_size
        dens_rows = lax.dynamic_slice_in_dim(density, row_first, block_size, 0)
        contrib = jnp.einsum(
            "mlp,ms->lsp",
            tile_block.reshape(block_size, block_size, aux_size),
            dens_rows,
            preferred_element_type=F32,
        )
        contrib = contrib.reshape(block_size, block_size * aux_size)
        target = left_lam[slot_index] * block_size
        current = lax.dynamic_slice_in_dim(running, target, block_size, 0)
        return lax.dynamic_update_slice_in_dim(running, current + contrib, target, 0)

    initial = jnp.zeros((window_rows, block_size * aux_size), F32)
    summed = lax.fori_loop(0, live_count, add_tile, initial)
    pattern_cols = jnp.repeat(back_pattern[:, 0], block_size).astype(F32)
    row_share = lax.psum_scatter(summed, "pair", scatter_dimension=0, tiled=True)
    applied = apply_metric(row_share, metric, aux_size)
    product = lax.dot_general(
        lax.all_gather(applied, "pair", axis=0, tiled=True),
        back_tiles,
        (((1,), (1,)), ((), ())),
        preferred_element_type=F32,
    )
    partial_exchange = product * pattern_cols[None, :]
    return lax.psum_scatter(partial_exchange, "col", scatter_dimension=0, tiled=True)


def encode(ref, index, value):
    width = value.shape[1]
    top = jnp.max(jnp.abs(value), axis=1, keepdims=True)
    power = jnp.floor(14.999 - jnp.log2(jnp.maximum(top, 1e-30)))
    power = jnp.minimum(power, 110.0)
    scaled = jnp.round(value * jnp.exp2(power))
    scaled = jnp.clip(scaled, -32767.0, 32767.0)
    ref[index + (slice(None), pl.ds(0, width))] = scaled.astype(jnp.int32).astype(I16)
    tail = jnp.broadcast_to(power, (value.shape[0], LANES))
    ref[index + (slice(None), pl.ds(width, LANES))] = tail.astype(jnp.int32).astype(I16)


def scale_of(ref, index, width):
    power = ref[index + (slice(None), pl.ds(width, LANES))]
    return jnp.exp2(-power.astype(jnp.int32).astype(F32))


def decode(ref, index, slab, scale):
    coded = ref[index + (slice(None), pl.ds(slab * LANES, LANES))]
    return coded.astype(jnp.int32).astype(F32) * scale


def left_kernel(row, lam, count, place, tile, dens, send, keep, total):
    slot = pl.program_id(0)
    block = tile.shape[1]

    @pl.when(slot == 0)
    def _():
        total[...] = jnp.zeros_like(total)

    @pl.when(slot < count[0])
    def _():
        first = pl.multiple_of((row[slot] // 2) * LANES, LANES)
        pair = dens[:, pl.ds(first, LANES)].astype(F32)
        rows = jnp.where(row[slot] % 2 == 1, pair[:, block:], pair[:, :block])
        where = lam[slot]
        total[where] += jnp.dot(rows.astype(BF16), tile[0], preferred_element_type=F32)

    @pl.when(slot == pl.num_programs(0) - 1)
    def _():
        inner = place[0]
        for outer in range(total.shape[0] // INNER):
            encode(send, (outer,), total[INNER * outer + 1 - inner])
            keep[outer] = total[INNER * outer + inner]


def inner_kernel(place, keep, got, own, *sends):
    width = keep.shape[2]

    def total(index):
        scale = scale_of(got, (index,), width)
        return [
            keep[index, :, pl.ds(s * LANES, LANES)] + decode(got, (index,), s, scale)
            for s in range(width // LANES)
        ]

    outer = place[1]
    for s, part in enumerate(total(outer)):
        own[:, pl.ds(s * LANES, LANES)] = part
    for step, send in enumerate(sends):
        index = jnp.bitwise_xor(outer, step + 1)
        encode(send, (), jnp.concatenate(total(index), axis=1))


def metric_kernel(own, *refs):
    *gots, metric, piece, turned, mixed = refs
    columns, width = own.shape
    slabs = width // LANES
    aux = LANES // 2
    scales = [scale_of(got, (), width) for got in gots]
    for s in range(slabs):
        value = own[:, pl.ds(s * LANES, LANES)]
        for got, scale in zip(gots, scales):
            value = value + decode(got, (), s, scale)
        turned[pl.ds(s, columns, stride=slabs), :] = value
    product = jnp.dot(
        turned[...], metric[...], precision=lax.Precision.HIGHEST, preferred_element_type=F32
    )
    product = product.reshape(columns // 2, 2, slabs, LANES)
    first = product[:, 0].reshape(columns // 2 * slabs, LANES)
    second = product[:, 1].reshape(columns // 2 * slabs, LANES)
    low = lax.broadcasted_iota(jnp.int32, first.shape, 1) < aux
    count = first.shape[0]
    mixed[pl.ds(0, count, stride=2), :] = jnp.where(low, first, pltpu.roll(second, aux, 1))
    mixed[pl.ds(1, count, stride=2), :] = jnp.where(low, pltpu.roll(first, aux, 1), second)
    piece[...] = mixed[...].reshape(piece.shape).astype(BF16)


def back_kernel(place, *refs):
    *pieces, back, pattern, keep, send, rows = refs
    groups, height, _ = pieces[0].shape
    half = rows.shape[0] // 2

    @pl.when(pl.program_id(0) == 0)
    def _():
        inner, outer, core = place[0], place[1], place[2]
        for i, piece in enumerate(pieces):
            holder = jnp.bitwise_xor(outer, i // INNER)
            across = jnp.bitwise_xor(inner, i % INNER)
            other = jnp.bitwise_xor(holder % 2, core)
            at = other * half + (holder // 2) * (half // 2) + across * height
            at = pl.multiple_of(at, height)
            for g in range(groups):
                rows[pl.ds(at, height), pl.ds(g * LANES, LANES)] = piece[g]

    product = lax.dot_general(
        rows[...], back[...], (((1,), (1,)), ((), ())), preferred_element_type=F32
    )
    product = product * pattern[...]
    keep[...] = product[:half]
    send[...] = product[half:].astype(BF16)


def whole(shape):
    return pl.BlockSpec(shape, lambda *_: (0,) * len(shape))


def params():
    return pltpu.CompilerParams(vmem_limit_bytes=56 << 20)


def pipelined(
    left_tiles, left_row, left_lam, left_count, density, metric, back_tiles, back_pattern,
    n_pair, n_col,
):
    slots, block, span = left_tiles.shape
    aux = span // block
    columns = density.shape[1]
    rows_held = back_tiles.shape[0]
    n_outer = n_pair // INNER
    height = block // CHUNKS
    width = height * aux
    coded = width + LANES
    groups = columns * aux // LANES

    here, col = lax.axis_index("pair"), lax.axis_index("col")
    inner, outer = here % INNER, here // INNER
    core, half_col = col % 2, col // 2
    place = jnp.stack([inner, outer, core]).astype(jnp.int32)
    dens = density.T
    zero = jnp.zeros_like(metric)
    metrics = jnp.block([[metric, zero], [zero, metric]])
    pattern = jnp.repeat(back_pattern[:, 0], block).astype(F32)[None, :]

    across = [(p, p ^ 1) for p in range(n_pair)]
    along = [
        [(p, ((p // INNER) ^ j) * INNER + p % INNER) for p in range(n_pair)]
        for j in range(n_outer)
    ]
    cores = [(c, c ^ 1) for c in range(n_col)]
    sides = [(c, c ^ 2) for c in range(n_col)]

    def left(k):
        return pl.pallas_call(
            left_kernel,
            grid_spec=pltpu.PrefetchScalarGridSpec(
                num_scalar_prefetch=4,
                grid=(slots,),
                in_specs=[
                    pl.BlockSpec(
                        (1, block, width),
                        lambda s, row, lam, count, place: (jnp.minimum(s, count[0] - 1), 0, k),
                    ),
                    whole(dens.shape),
                ],
                out_specs=[whole((n_outer, columns, coded)), whole((n_outer, columns, width))],
                scratch_shapes=[pltpu.VMEM((LW, columns, width), F32)],
            ),
            out_shape=[
                jax.ShapeDtypeStruct((n_outer, columns, coded), I16),
                jax.ShapeDtypeStruct((n_outer, columns, width), F32),
            ],
            compiler_params=params(),
            cost_estimate=pl.CostEstimate(
                flops=2 * slots * columns * block * width,
                bytes_accessed=slots * block * width * 2 + n_outer * columns * width * 6,
                transcendentals=0,
            ),
            name="left",
        )(left_row, left_lam, left_count, place, left_tiles, dens)

    def join(keep, got):
        return pl.pallas_call(
            inner_kernel,
            in_specs=[
                pl.BlockSpec(memory_space=pltpu.SMEM),
                pl.BlockSpec(memory_space=pltpu.VMEM),
                pl.BlockSpec(memory_space=pltpu.VMEM),
            ],
            out_specs=[pl.BlockSpec(memory_space=pltpu.VMEM)] * n_outer,
            out_shape=[jax.ShapeDtypeStruct((columns, width), F32)]
            + [jax.ShapeDtypeStruct((columns, coded), I16)] * (n_outer - 1),
            compiler_params=params(),
            cost_estimate=pl.CostEstimate(
                flops=n_outer * columns * width * 8,
                bytes_accessed=n_outer * columns * width * 8,
                transcendentals=0,
            ),
            name="join",
        )(place, keep, got)

    def finish(own, gots):
        return pl.pallas_call(
            metric_kernel,
            out_shape=jax.ShapeDtypeStruct((groups, height, LANES), BF16),
            scratch_shapes=[
                pltpu.VMEM((columns * width // LANES, LANES), F32),
                pltpu.VMEM((columns * width // LANES, LANES), F32),
            ],
            compiler_params=params(),
            cost_estimate=pl.CostEstimate(
                flops=columns * width * 2 * LANES * 6,
                bytes_accessed=columns * width * 12,
                transcendentals=0,
            ),
            name="metric",
        )(own, *gots, metrics)

    step = 512 if rows_held % 512 == 0 else LANES

    def back(pieces):
        lines = n_pair * height
        return pl.pallas_call(
            back_kernel,
            grid_spec=pltpu.PrefetchScalarGridSpec(
                num_scalar_prefetch=1,
                grid=(rows_held // step,),
                in_specs=[whole(piece.shape) for piece in pieces]
                + [
                    pl.BlockSpec((step, columns * aux), lambda i, place: (i, 0)),
                    pl.BlockSpec((1, step), lambda i, place: (0, i)),
                ],
                out_specs=[pl.BlockSpec((lines // 2, step), lambda i, place: (0, i))] * 2,
                scratch_shapes=[pltpu.VMEM((lines, columns * aux), BF16)],
            ),
            out_shape=[
                jax.ShapeDtypeStruct((lines // 2, rows_held), F32),
                jax.ShapeDtypeStruct((lines // 2, rows_held), BF16),
            ],
            compiler_params=params(),
            cost_estimate=pl.CostEstimate(
                flops=2 * lines * rows_held * columns * aux,
                bytes_accessed=rows_held * columns * aux * 2,
                transcendentals=0,
            ),
            name="back",
        )(place, *pieces, back_tiles, pattern)

    outs = []
    for k in range(CHUNKS):
        send, keep = left(k)
        got = lax.ppermute(send, "pair", across)
        own, *sends = join(keep, got)
        gots = [lax.ppermute(s, "pair", along[j + 1]) for j, s in enumerate(sends)]
        piece = finish(own, gots)
        held = [piece] + [lax.ppermute(piece, "pair", along[j]) for j in range(1, n_outer)]
        pieces = []
        for h in held:
            pieces += [h, lax.ppermute(h, "pair", across)]
        mine, theirs = back(pieces)
        partner = lax.ppermute(theirs, "col", cores)
        mine = mine.reshape(2, -1, rows_held)
        partner = partner.reshape(2, -1, rows_held)

        def pick(i):
            return lax.dynamic_index_in_dim(mine, i, 0, False) + lax.dynamic_index_in_dim(
                partner, i, 0, False
            ).astype(F32)

        far = lax.ppermute(pick(1 - half_col).astype(BF16), "col", sides)
        outs.append((pick(half_col) + far.astype(F32)).reshape(INNER, height, rows_held))
    out = outs[0] if CHUNKS == 1 else jnp.concatenate(outs, axis=1)
    return out.reshape(INNER * block, rows_held)


def solution(mesh):
    placed = (
        P("pair", None, None),
        P("pair"),
        P("pair"),
        P("pair"),
        P("pair", "col"),
        P(),
        P("pair", "col"),
        P("pair", "col"),
    )
    n_pair, n_col = mesh.shape["pair"], mesh.shape["col"]

    def per_device(*args):
        block, span = args[0].shape[1:]
        fits = (
            n_pair == LW
            and n_col == 4
            and n_pair == INNER * n_col
            and 2 * (span // block) == LANES
            and args[4].shape[0] % LANES == 0
            and 2 * block == LANES
        )
        if not fits:
            return general(*args)
        return pipelined(*args, n_pair, n_col)

    return jax.shard_map(
        per_device, mesh=mesh, in_specs=placed, out_specs=P("col", "pair"), check_vma=False
    )
```
